768 devices in a mesh: section: 16 (over x, y_hi), tp: 48 (over y_lo, z, core).
Axes of the slice: x: 4, y: 8 (y_hi: 4, y_lo: 2; y = y_hi * 2 + y_lo), z: 12, core: 2. Of those that a mesh axis runs over, the one named last changes fastest.
Arguments:
- queries_now: bfloat16 [16, 6144, 4096], P('section', 'tp'), may hold values from -6 to 6
- stash_now: bfloat16 [16, 6144, 1024], P('section', 'tp'), may hold values from -6 to 6
- positions_now: int32 [16, 6144], P('section', 'tp'), may hold values from 0 to 127, as said below
- queries_old: bfloat16 [16, 6144, 4096], P('section', 'tp'), may hold values from -6 to 6
- positions_old: int32 [16, 6144], P('section', 'tp'), may hold values from 0 to 127, as said below
- stash_kept: bfloat16 [16, 3072, 1024], P('section', 'tp'), may hold values from -6 to 6
- stash_held: bfloat16 [16, 3072, 1024], P('section', 'tp'), may hold values from -6 to 6
Outputs:
- mixed_now: bfloat16 [16, 6144, 4096], P('section', 'tp')
- mixed_old: bfloat16 [16, 6144, 4096], P('section', 'tp')
- stash_stored: bfloat16 [16, 3072, 1024], P('section', 'tp')
The draws below stay inside these ranges and needn't reach their ends.
Inputs may be any that keep to these rules, and one draw needn't show every extreme that they name: `positions_now`: positions restart at 0 at the first token of each reaction and rise by one within it; a reaction has at most 128 tokens. `positions_old`: positions restart at 0 at the first token of each reaction and rise by one within it; a reaction has at most 128 tokens.
All inputs are finite; a program needn't handle non-finite values.
Results may differ from the reference program's by a relative error of at most 0.003.
Values may be sent and summed in bfloat16 or wider, within the bound.
A program may use at most 32 MiB of HBM per device.

```python
import jax
import jax.numpy as jnp
from jax import lax

KV_HEADS = 4
HEAD_DIM = 128
TOK_DEV = 128
SECTIONS = 16
SEQ = 6144
EVICT = 64
DOC_MAX = 128
GROUP = 8
Q_WIDTH = 4096
KV_WIDTH = 512


def reaction_positions(key):
    lengths = jax.random.randint(key, (SECTIONS, SEQ), 1, DOC_MAX + 1).astype(jnp.int32)
    lengths = lengths.at[:, 0].set(TOK_DEV // 2)
    lengths = lengths.at[:, 1].set(DOC_MAX)
    starts = jnp.cumsum(lengths, axis=1) - lengths
    section_rows = jnp.broadcast_to(jnp.arange(SECTIONS, dtype=jnp.int32)[:, None], (SECTIONS, SEQ))
    flags = jnp.where(starts < SEQ, 1, 0).astype(jnp.int32)
    marks = jnp.zeros((SECTIONS, SEQ), jnp.int32).at[section_rows, jnp.minimum(starts, SEQ - 1)].max(flags)
    index = jnp.broadcast_to(jnp.arange(SEQ, dtype=jnp.int32)[None, :], (SECTIONS, SEQ))
    latest = lax.cummax(jnp.where(marks > 0, index, 0), axis=1)
    return (index - latest).astype(jnp.int32)


def attention_inputs(key):
    key_query, key_keys, key_values = jax.random.split(key, 3)
    query_shape = (SECTIONS, SEQ, KV_HEADS, GROUP, HEAD_DIM)
    key_shape = (SECTIONS, SEQ, KV_HEADS, HEAD_DIM)
    queries = jnp.clip(jax.random.normal(key_query, query_shape, jnp.float32), -6.0, 6.0)
    key_rows = jnp.clip(jax.random.normal(key_keys, key_shape, jnp.float32), -6.0, 6.0)
    value_rows = jnp.clip(jax.random.normal(key_values, key_shape, jnp.float32), -6.0, 6.0)
    stash = jnp.concatenate([key_rows.reshape(SECTIONS, SEQ, KV_WIDTH), value_rows.reshape(SECTIONS, SEQ, KV_WIDTH)], -1)
    return (queries.reshape(SECTIONS, SEQ, Q_WIDTH), stash)


def draw_queries_now(key, part):
    return attention_inputs(jax.random.fold_in(key, 21))[0].astype(jnp.bfloat16)


def draw_stash_now(key, part):
    return attention_inputs(jax.random.fold_in(key, 21))[1].astype(jnp.bfloat16)


def draw_positions_now(key, part):
    return reaction_positions(jax.random.fold_in(key, 11))


def draw_queries_old(key, part):
    return attention_inputs(jax.random.fold_in(key, 22))[0].astype(jnp.bfloat16)


def draw_positions_old(key, part):
    return reaction_positions(jax.random.fold_in(key, 12))


def older_blocks(key):
    stash = attention_inputs(jax.random.fold_in(key, 22))[1]
    return stash.reshape(SECTIONS, SEQ // TOK_DEV, TOK_DEV, 2 * KV_WIDTH)


def draw_stash_kept(key, part):
    blocks = older_blocks(key)
    return blocks[:, :, :EVICT].reshape(SECTIONS, SEQ // 2, 2 * KV_WIDTH).astype(jnp.bfloat16)


def draw_stash_held(key, part):
    blocks = older_blocks(key)
    return blocks[::-1, :, EVICT:].reshape(SECTIONS, SEQ // 2, 2 * KV_WIDTH).astype(jnp.bfloat16)


def setup_inputs(seed: int = 0) -> dict:
    key_of = jax.random.split(jax.random.key(seed), 8)
    return {
        "queries_now": draw_queries_now(jax.random.fold_in(key_of[7], 71), 0),
        "stash_now": draw_stash_now(jax.random.fold_in(key_of[7], 71), 0),
        "positions_now": draw_positions_now(jax.random.fold_in(key_of[7], 71), 0),
        "queries_old": draw_queries_old(jax.random.fold_in(key_of[7], 71), 0),
        "positions_old": draw_positions_old(jax.random.fold_in(key_of[7], 71), 0),
        "stash_kept": draw_stash_kept(jax.random.fold_in(key_of[7], 71), 0),
        "stash_held": draw_stash_held(jax.random.fold_in(key_of[7], 71), 0),
    }


def block_attention(queries, prior, resident, positions):
    row_count = queries.shape[0]
    joined = jnp.concatenate([prior, resident], 0).astype(jnp.float32)
    key_rows = joined[:, :KV_WIDTH].reshape(2 * row_count, KV_HEADS, HEAD_DIM)
    value_rows = joined[:, KV_WIDTH:].reshape(2 * row_count, KV_HEADS, HEAD_DIM)
    grouped = queries.astype(jnp.float32).reshape(row_count, KV_HEADS, GROUP, HEAD_DIM)
    scores = jnp.einsum('tkgd,skd->kgts', grouped, key_rows) * (HEAD_DIM ** -0.5)
    query_index = jnp.arange(row_count, dtype=jnp.int32)
    key_index = jnp.arange(2 * row_count, dtype=jnp.int32) - row_count
    visible = (key_index[None, :] <= query_index[:, None]) & (key_index[None, :] >= (query_index - positions)[:, None])
    scores = jnp.where(visible, scores, -1e30)
    row_peak = jnp.max(scores, axis=-1, keepdims=True)
    raised = jnp.exp(scores - row_peak)
    row_total = jnp.sum(raised, axis=-1)
    weights = lax.optimization_barrier(raised.astype(jnp.bfloat16)).astype(jnp.float32)
    summed = jnp.einsum('kgts,skd->tkgd', weights, value_rows)
    result = summed / jnp.transpose(row_total, (2, 0, 1))[..., None]
    return result.astype(jnp.bfloat16).reshape(row_count, Q_WIDTH)


def attend(queries, stash, positions):
    blocks = SEQ // TOK_DEV
    width = 2 * KV_WIDTH
    stash_blocks = stash.reshape(SECTIONS, blocks, TOK_DEV, width)
    prior = jnp.concatenate([jnp.zeros_like(stash_blocks[:, :1]), stash_blocks[:, :-1]], axis=1)
    def one_block(items):
        return block_attention(items[0], items[1], items[2], items[3])
    mixed = lax.map(one_block, (queries.reshape(SECTIONS * blocks, TOK_DEV, Q_WIDTH),
                                prior.reshape(SECTIONS * blocks, TOK_DEV, width),
                                stash_blocks.reshape(SECTIONS * blocks, TOK_DEV, width),
                                positions.reshape(SECTIONS * blocks, TOK_DEV)))
    return mixed.reshape(SECTIONS, SEQ, Q_WIDTH)


def reference(queries_now, stash_now, positions_now, queries_old, positions_old, stash_kept, stash_held):
    blocks = SEQ // TOK_DEV
    width = 2 * KV_WIDTH
    kept_blocks = stash_kept.reshape(SECTIONS, blocks, EVICT, width)
    held_blocks = stash_held.reshape(SECTIONS, blocks, EVICT, width)[::-1]
    stash_old = jnp.concatenate([kept_blocks, held_blocks], axis=2).reshape(SECTIONS, SEQ, width)
    mixed_now = attend(queries_now, stash_now, positions_now)
    mixed_old = attend(queries_old, stash_old, positions_old)
    stash_stored = stash_now.reshape(SECTIONS, blocks, TOK_DEV, width)[::-1, :, EVICT:].reshape(SECTIONS, blocks * EVICT, width)
    return mixed_now, mixed_old, stash_stored
```

```python
import functools
import math

import jax
import jax.numpy as jnp
from jax import lax
from jax.experimental import pallas as pl
from jax.experimental.pallas import tpu as pltpu
from jax.sharding import PartitionSpec as P

KV_HEADS = 4
HEAD_DIM = 128
GROUP = 8
KV_WIDTH = KV_HEADS * HEAD_DIM
CHUNKS = 4
HEADS_DOT = 4
MESH = pl.DeviceIdType.MESH
NEG = -1e30


def mask_rows(positions, rows):
    key = lax.broadcasted_iota(jnp.int32, (2 * rows, rows), 0) - rows
    query = lax.broadcasted_iota(jnp.int32, (2 * rows, rows), 1)
    visible = (key <= query) & (key >= query - positions)
    return jnp.where(visible, 0.0, NEG).astype(jnp.bfloat16)


def attend_head(head, q_ref, kv_ref, mask_ref, eye_ref, out_ref):
    rows = q_ref.shape[0]
    factor = HEAD_DIM ** (-0.5) * math.log2(math.e)
    key_col = pl.multiple_of(head * HEAD_DIM, HEAD_DIM)
    value_col = pl.multiple_of(KV_WIDTH + head * HEAD_DIM, HEAD_DIM)
    keys = jnp.concatenate([kv_ref[:, pl.ds(key_col, HEAD_DIM)], mask_ref[...]], 1)
    values = jnp.concatenate(
        [kv_ref[:, pl.ds(value_col, HEAD_DIM)], jnp.ones((2 * rows, HEAD_DIM), jnp.bfloat16)], 1
    )
    eye = eye_ref[...]
    for first in range(0, GROUP, HEADS_DOT):
        cols = [
            pl.multiple_of(head * GROUP * HEAD_DIM + (first + g) * HEAD_DIM, HEAD_DIM)
            for g in range(HEADS_DOT)
        ]
        queries = jnp.concatenate(
            [jnp.concatenate([q_ref[:, pl.ds(c, HEAD_DIM)], eye], 1) for c in cols], 0
        )
        scores = lax.dot_general(
            queries, keys, (((1,), (1,)), ((), ())), preferred_element_type=jnp.float32
        )
        peak = jnp.max(scores, axis=1, keepdims=True)
        weights = jnp.exp2((scores - peak) * factor).astype(jnp.bfloat16)
        summed = jnp.dot(weights, values, preferred_element_type=jnp.float32)
        mixed = (summed[:, :HEAD_DIM] / summed[:, HEAD_DIM:]).astype(jnp.bfloat16)
        for g, c in enumerate(cols):
            out_ref[:, pl.ds(c, HEAD_DIM)] = mixed[g * rows : (g + 1) * rows]


def kernel(
    q_now, stash_now, pos_now, q_old, pos_old, kept, held,
    mixed_now, mixed_old, stored,
    qn, qo, on, oo, kv_now, kv_old, mask_now, mask_old, eye,
    load_sem, out_sem, send_sem, recv_sem,
):
    rows = stash_now.shape[0]
    half = kept.shape[0]
    part = half // CHUNKS
    sections = lax.axis_size("section")
    count = lax.axis_size("tp")
    s = lax.axis_index("section")
    t = lax.axis_index("tp")
    mirror = {"section": sections - 1 - s}
    right = {"tp": t + 1}
    has_right = t < count - 1
    has_left = t > 0

    loads = [
        pltpu.make_async_copy(stash_now, kv_now.at[pl.ds(rows, rows)], load_sem.at[0]),
        pltpu.make_async_copy(q_now, qn, load_sem.at[1]),
        pltpu.make_async_copy(kept, kv_old.at[pl.ds(rows, half)], load_sem.at[2]),
        pltpu.make_async_copy(q_old, qo, load_sem.at[3]),
    ]
    for load in loads:
        load.start()

    barrier = pltpu.get_barrier_semaphore()
    pl.semaphore_signal(barrier, inc=1, device_id=mirror, device_id_type=MESH)

    @pl.when(has_right)
    def _():
        pl.semaphore_signal(barrier, inc=1, device_id=right, device_id_type=MESH)

    @pl.when(has_left)
    def _():
        pl.semaphore_signal(barrier, inc=1, device_id={"tp": t - 1}, device_id_type=MESH)

    pl.semaphore_wait(
        barrier, 1 + has_right.astype(jnp.int32) + has_left.astype(jnp.int32)
    )

    def remote(index, src, dst, device):
        return pltpu.make_async_remote_copy(
            src_ref=src, dst_ref=dst, send_sem=send_sem.at[index], recv_sem=recv_sem.at[index],
            device_id=device, device_id_type=MESH,
        )

    swap = [
        remote(
            c, held.at[pl.ds(c * part, part)],
            kv_old.at[pl.ds(rows + half + c * part, part)], mirror,
        )
        for c in range(CHUNKS)
    ]
    pass_on = [
        remote(
            CHUNKS + c, kv_old.at[pl.ds(rows + half + c * part, part)],
            kv_old.at[pl.ds(half + c * part, part)], right,
        )
        for c in range(CHUNKS)
    ]
    shift_now = remote(2 * CHUNKS, stash_now, kv_now.at[pl.ds(0, rows)], right)
    shift_kept = remote(2 * CHUNKS + 1, kept, kv_old.at[pl.ds(0, half)], right)
    evict = remote(2 * CHUNKS + 2, stash_now.at[pl.ds(rows - half, half)], stored, mirror)

    for copy in swap:
        copy.start()

    @pl.when(has_right)
    def _():
        shift_now.start()
        shift_kept.start()

    evict.start()

    @pl.when(jnp.logical_not(has_left))
    def _():
        kv_now[pl.ds(0, rows), :] = jnp.zeros((rows, 2 * KV_WIDTH), jnp.bfloat16)
        kv_old[pl.ds(0, rows), :] = jnp.zeros((rows, 2 * KV_WIDTH), jnp.bfloat16)

    eye[...] = jnp.where(
        lax.broadcasted_iota(jnp.int32, (rows, rows), 0)
        == lax.broadcasted_iota(jnp.int32, (rows, rows), 1),
        1.0, 0.0,
    ).astype(jnp.bfloat16)
    mask_now[...] = mask_rows(pos_now[...], rows)
    mask_old[...] = mask_rows(pos_old[...], rows)

    loads[0].wait()
    loads[1].wait()

    @pl.when(has_left)
    def _():
        shift_now.wait_recv()

    width = GROUP * HEAD_DIM

    def flush(out_v, out_h, head, index):
        col = pl.multiple_of(head * width, width)
        return pltpu.make_async_copy(
            out_v.at[:, pl.ds(col, width)], out_h.at[:, pl.ds(col, width)], out_sem.at[index]
        )

    for head in range(KV_HEADS):
        attend_head(head, qn, kv_now, mask_now, eye, on)
        flush(on, mixed_now, head, head).start()
        for c in range(head * CHUNKS // KV_HEADS, (head + 1) * CHUNKS // KV_HEADS):
            swap[c].wait_recv()

            @pl.when(has_right)
            def _(c=c):
                pass_on[c].start()

    loads[2].wait()
    loads[3].wait()

    @pl.when(has_left)
    def _():
        shift_kept.wait_recv()
        for copy in pass_on:
            copy.wait_recv()

    for head in range(KV_HEADS):
        attend_head(head, qo, kv_old, mask_old, eye, oo)
        flush(oo, mixed_old, head, KV_HEADS + head).start()

    for head in range(KV_HEADS):
        flush(on, mixed_now, head, head).wait()
        flush(oo, mixed_old, head, KV_HEADS + head).wait()

    for copy in swap:
        copy.wait_send()

    @pl.when(has_right)
    def _():
        shift_now.wait_send()
        shift_kept.wait_send()
        for copy in pass_on:
            copy.wait_send()

    evict.wait()


def body(queries_now, stash_now, positions_now, queries_old, positions_old, stash_kept, stash_held):
    rows, width = queries_now.shape[1:]
    half, kv_width = stash_kept.shape[1:]
    bf16 = jnp.bfloat16
    hbm = pl.BlockSpec(memory_space=pl.ANY)
    vmem = pl.BlockSpec(memory_space=pltpu.VMEM)
    remote_count = 2 * CHUNKS + 3
    mixed_now, mixed_old, stored = pl.pallas_call(
        kernel,
        out_shape=(
            jax.ShapeDtypeStruct((rows, width), bf16),
            jax.ShapeDtypeStruct((rows, width), bf16),
            jax.ShapeDtypeStruct((half, kv_width), bf16),
        ),
        in_specs=[hbm, hbm, vmem, hbm, vmem, hbm, hbm],
        out_specs=(hbm, hbm, hbm),
        scratch_shapes=[
            pltpu.VMEM((rows, width), bf16),
            pltpu.VMEM((rows, width), bf16),
            pltpu.VMEM((rows, width), bf16),
            pltpu.VMEM((rows, width), bf16),
            pltpu.VMEM((2 * rows, kv_width), bf16),
            pltpu.VMEM((2 * rows, kv_width), bf16),
            pltpu.VMEM((2 * rows, rows), bf16),
            pltpu.VMEM((2 * rows, rows), bf16),
            pltpu.VMEM((rows, rows), bf16),
            pltpu.SemaphoreType.DMA((4,)),
            pltpu.SemaphoreType.DMA((2 * KV_HEADS,)),
            pltpu.SemaphoreType.DMA((remote_count,)),
            pltpu.SemaphoreType.DMA((remote_count,)),
        ],
        compiler_params=pltpu.CompilerParams(collective_id=0, has_side_effects=True),
        name="relay_attention",
    )(
        queries_now[0], stash_now[0], positions_now, queries_old[0], positions_old,
        stash_kept[0], stash_held[0],
    )
    return (mixed_now[None], mixed_old[None], stored[None])


def solution(mesh):
    return jax.shard_map(
        body,
        mesh=mesh,
        in_specs=(
            P("section", "tp", None),
            P("section", "tp", None),
            P("section", "tp"),
            P("section", "tp", None),
            P("section", "tp"),
            P("section", "tp", None),
            P("section", "tp", None),
        ),
        out_specs=(P("section", "tp", None), P("section", "tp", None), P("section", "tp", None)),
        check_vma=False,
    )
```

```python
import functools
import math

import jax
import jax.numpy as jnp
from jax import lax
from jax.experimental import pallas as pl
from jax.experimental.pallas import tpu as pltpu
from jax.sharding import PartitionSpec as P

KV_HEADS = 4
HEAD_DIM = 128
GROUP = 8
KV_WIDTH = KV_HEADS * HEAD_DIM
CHUNKS = 4
HEADS_DOT = 4
MESH = pl.DeviceIdType.MESH
NEG = -1e30


def mask_rows(positions, rows):
    key = lax.broadcasted_iota(jnp.int32, (2 * rows, rows), 0) - rows
    query = lax.broadcasted_iota(jnp.int32, (2 * rows, rows), 1)
    visible = (key <= query) & (key >= query - positions)
    return jnp.where(visible, 0.0, NEG).astype(jnp.bfloat16)


def attend_head(head, q_ref, kv_ref, mask_ref, eye_ref, out_ref):
    rows = q_ref.shape[0]
    factor = HEAD_DIM ** (-0.5) * math.log2(math.e)
    key_col = pl.multiple_of(head * HEAD_DIM, HEAD_DIM)
    value_col = pl.multiple_of(KV_WIDTH + head * HEAD_DIM, HEAD_DIM)
    keys = jnp.concatenate([kv_ref[:, pl.ds(key_col, HEAD_DIM)], mask_ref[...]], 1)
    values = jnp.concatenate(
        [kv_ref[:, pl.ds(value_col, HEAD_DIM)], jnp.ones((2 * rows, HEAD_DIM), jnp.bfloat16)], 1
    )
    eye = eye_ref[...]
    for first in range(0, GROUP, HEADS_DOT):
        cols = [
            pl.multiple_of(head * GROUP * HEAD_DIM + (first + g) * HEAD_DIM, HEAD_DIM)
            for g in range(HEADS_DOT)
        ]
        queries = jnp.concatenate(
            [jnp.concatenate([q_ref[:, pl.ds(c, HEAD_DIM)], eye], 1) for c in cols], 0
        )
        scores = lax.dot_general(
            queries, keys, (((1,), (1,)), ((), ())), preferred_element_type=jnp.float32
        )
        peak = jnp.max(scores, axis=1, keepdims=True)
        weights = jnp.exp2((scores - peak) * factor).astype(jnp.bfloat16)
        summed = jnp.dot(weights, values, preferred_element_type=jnp.float32)
        mixed = (summed[:, :HEAD_DIM] / summed[:, HEAD_DIM:]).astype(jnp.bfloat16)
        for g, c in enumerate(cols):
            out_ref[:, pl.ds(c, HEAD_DIM)] = mixed[g * rows : (g + 1) * rows]


def kernel(
    q_now, stash_now, pos_now, q_old, pos_old, kept, held,
    mixed_now, mixed_old, stored,
    qn, qo, kv_now, kv_old, mask_now, mask_old, eye,
    load_sem, send_sem, recv_sem,
):
    rows = stash_now.shape[0]
    half = kept.shape[0]
    part = half // CHUNKS
    sections = lax.axis_size("section")
    count = lax.axis_size("tp")
    s = lax.axis_index("section")
    t = lax.axis_index("tp")
    mirror = {"section": sections - 1 - s}
    right = {"tp": t + 1}
    has_right = t < count - 1
    has_left = t > 0
    seam = count // 2
    gives_direct = t == seam - 1
    takes_direct = t == seam
    forwards_first = (t == 0) | (t == seam)
    passes_on = has_right & jnp.logical_not(gives_direct)
    takes_passed = has_left & jnp.logical_not(takes_direct)

    loads = [
        pltpu.make_async_copy(stash_now, kv_now.at[pl.ds(rows, rows)], load_sem.at[0]),
        pltpu.make_async_copy(q_now, qn, load_sem.at[1]),
        pltpu.make_async_copy(kept, kv_old.at[pl.ds(rows, half)], load_sem.at[2]),
        pltpu.make_async_copy(q_old, qo, load_sem.at[3]),
    ]
    for load in loads:
        load.start()

    barrier = pltpu.get_barrier_semaphore()
    pl.semaphore_signal(barrier, inc=1, device_id=mirror, device_id_type=MESH)

    @pl.when(has_left)
    def _():
        pl.semaphore_signal(barrier, inc=1, device_id={"tp": t - 1}, device_id_type=MESH)

    @pl.when(takes_direct)
    def _():
        pl.semaphore_signal(
            barrier, inc=1, device_id={"section": sections - 1 - s, "tp": t - 1}, device_id_type=MESH
        )

    pl.semaphore_wait(
        barrier, 1 + has_right.astype(jnp.int32) + gives_direct.astype(jnp.int32)
    )

    def remote(index, src, dst, device):
        return pltpu.make_async_remote_copy(
            src_ref=src, dst_ref=dst, send_sem=send_sem.at[index], recv_sem=recv_sem.at[index],
            device_id=device, device_id_type=MESH,
        )

    swap = [
        remote(
            c, held.at[pl.ds(c * part, part)],
            kv_old.at[pl.ds(rows + half + c * part, part)], mirror,
        )
        for c in range(CHUNKS)
    ]
    pass_on = [
        remote(
            CHUNKS + c, kv_old.at[pl.ds(rows + half + c * part, part)],
            kv_old.at[pl.ds(half + c * part, part)], right,
        )
        for c in range(CHUNKS)
    ]
    shift_now = remote(2 * CHUNKS, stash_now, kv_now.at[pl.ds(0, rows)], right)
    shift_kept = remote(2 * CHUNKS + 1, kept, kv_old.at[pl.ds(0, half)], right)
    direct = remote(
        2 * CHUNKS + 3, held, kv_old.at[pl.ds(half, half)],
        {"section": sections - 1 - s, "tp": t + 1},
    )
    evict = remote(2 * CHUNKS + 2, stash_now.at[pl.ds(rows - half, half)], stored, mirror)

    for copy in swap:
        copy.start()

    @pl.when(has_right)
    def _():
        shift_now.start()
        shift_kept.start()

    @pl.when(gives_direct)
    def _():
        direct.start()

    evict.start()

    @pl.when(jnp.logical_not(has_left))
    def _():
        kv_now[pl.ds(0, rows), :] = jnp.zeros((rows, 2 * KV_WIDTH), jnp.bfloat16)
        kv_old[pl.ds(0, rows), :] = jnp.zeros((rows, 2 * KV_WIDTH), jnp.bfloat16)

    eye[...] = jnp.where(
        lax.broadcasted_iota(jnp.int32, (rows, rows), 0)
        == lax.broadcasted_iota(jnp.int32, (rows, rows), 1),
        1.0, 0.0,
    ).astype(jnp.bfloat16)
    mask_now[...] = mask_rows(pos_now[...], rows)
    mask_old[...] = mask_rows(pos_old[...], rows)

    @pl.when(forwards_first)
    def _():
        for c in range(CHUNKS):
            swap[c].wait_recv()
            pass_on[c].start()

    loads[0].wait()
    loads[1].wait()

    @pl.when(has_left)
    def _():
        shift_now.wait_recv()

    for head in range(KV_HEADS):
        attend_head(head, qn, kv_now, mask_now, eye, mixed_now)
        for c in range(head * CHUNKS // KV_HEADS, (head + 1) * CHUNKS // KV_HEADS):

            @pl.when(jnp.logical_not(forwards_first))
            def _(c=c):
                swap[c].wait_recv()

            @pl.when(passes_on & jnp.logical_not(forwards_first))
            def _(c=c):
                pass_on[c].start()

    loads[2].wait()
    loads[3].wait()

    @pl.when(has_left)
    def _():
        shift_kept.wait_recv()

    @pl.when(takes_passed)
    def _():
        for copy in pass_on:
            copy.wait_recv()

    @pl.when(takes_direct)
    def _():
        direct.wait_recv()

    for head in range(KV_HEADS):
        attend_head(head, qo, kv_old, mask_old, eye, mixed_old)

    for copy in swap:
        copy.wait_send()

    @pl.when(has_right)
    def _():
        shift_now.wait_send()
        shift_kept.wait_send()

    @pl.when(passes_on)
    def _():
        for copy in pass_on:
            copy.wait_send()

    @pl.when(gives_direct)
    def _():
        direct.wait_send()

    evict.wait()


def write_out(now_in, old_in, stored_in, now_out, old_out, stored_out, sem):
    copies = [
        pltpu.make_async_copy(now_in, now_out, sem.at[0]),
        pltpu.make_async_copy(old_in, old_out, sem.at[1]),
        pltpu.make_async_copy(stored_in, stored_out, sem.at[2]),
    ]
    for copy in copies:
        copy.start()
    for copy in copies:
        copy.wait()


def body(queries_now, stash_now, positions_now, queries_old, positions_old, stash_kept, stash_held):
    rows, width = queries_now.shape[1:]
    half, kv_width = stash_kept.shape[1:]
    bf16 = jnp.bfloat16
    hbm = pl.BlockSpec(memory_space=pl.ANY)
    vmem = pl.BlockSpec(memory_space=pltpu.VMEM)
    remote_count = 2 * CHUNKS + 4
    mixed_now, mixed_old, stored = pl.pallas_call(
        kernel,
        out_shape=(
            pltpu.VMEM((rows, width), bf16),
            pltpu.VMEM((rows, width), bf16),
            pltpu.VMEM((half, kv_width), bf16),
        ),
        in_specs=[hbm, hbm, vmem, hbm, vmem, hbm, hbm],
        out_specs=(vmem, vmem, vmem),
        scratch_shapes=[
            pltpu.VMEM((rows, width), bf16),
            pltpu.VMEM((rows, width), bf16),
            pltpu.VMEM((2 * rows, kv_width), bf16),
            pltpu.VMEM((2 * rows, kv_width), bf16),
            pltpu.VMEM((2 * rows, rows), bf16),
            pltpu.VMEM((2 * rows, rows), bf16),
            pltpu.VMEM((rows, rows), bf16),
            pltpu.SemaphoreType.DMA((4,)),
            pltpu.SemaphoreType.DMA((remote_count,)),
            pltpu.SemaphoreType.DMA((remote_count,)),
        ],
        compiler_params=pltpu.CompilerParams(collective_id=0, has_side_effects=True),
        name="relay_attention",
    )(
        queries_now[0], stash_now[0], positions_now, queries_old[0], positions_old,
        stash_kept[0], stash_held[0],
    )
    shapes = tuple(jax.ShapeDtypeStruct(a.shape, a.dtype) for a in (mixed_now, mixed_old, stored))
    mixed_now, mixed_old, stored = pl.pallas_call(
        write_out,
        out_shape=shapes,
        in_specs=[pl.BlockSpec(memory_space=pl.ANY)] * 3,
        out_specs=(hbm, hbm, hbm),
        scratch_shapes=[pltpu.SemaphoreType.DMA((3,))],
        compiler_params=pltpu.CompilerParams(vmem_limit_bytes=2**20),
        name="write_out",
    )(mixed_now, mixed_old, stored)
    return (mixed_now[None], mixed_old[None], stored[None])


def solution(mesh):
    return jax.shard_map(
        body,
        mesh=mesh,
        in_specs=(
            P("section", "tp", None),
            P("section", "tp", None),
            P("section", "tp"),
            P("section", "tp", None),
            P("section", "tp"),
            P("section", "tp", None),
            P("section", "tp", None),
        ),
        out_specs=(P("section", "tp", None), P("section", "tp", None), P("section", "tp", None)),
        check_vma=False,
    )
```

```python
import functools
import math

import jax
import jax.numpy as jnp
from jax import lax
from jax.experimental import pallas as pl
from jax.experimental.pallas import tpu as pltpu
from jax.sharding import PartitionSpec as P

KV_HEADS = 4
HEAD_DIM = 128
GROUP = 8
KV_WIDTH = KV_HEADS * HEAD_DIM
CHUNKS = 4
HEADS_DOT = 4
MESH = pl.DeviceIdType.MESH
NEG = -1e30


def mask_rows(positions, rows):
    key = lax.broadcasted_iota(jnp.int32, (2 * rows, rows), 0) - rows
    query = lax.broadcasted_iota(jnp.int32, (2 * rows, rows), 1)
    visible = (key <= query) & (key >= query - positions)
    return jnp.where(visible, 0.0, NEG).astype(jnp.bfloat16)


def attend_head(head, q_ref, kv_ref, mask_ref, eye_ref, out_ref):
    rows = q_ref.shape[0]
    factor = HEAD_DIM ** (-0.5) * math.log2(math.e)
    key_col = pl.multiple_of(head * HEAD_DIM, HEAD_DIM)
    value_col = pl.multiple_of(KV_WIDTH + head * HEAD_DIM, HEAD_DIM)
    keys = jnp.concatenate([kv_ref[:, pl.ds(key_col, HEAD_DIM)], mask_ref[...]], 1)
    values = jnp.concatenate(
        [kv_ref[:, pl.ds(value_col, HEAD_DIM)], jnp.ones((2 * rows, HEAD_DIM), jnp.bfloat16)], 1
    )
    eye = eye_ref[...]
    for first in range(0, GROUP, HEADS_DOT):
        cols = [
            pl.multiple_of(head * GROUP * HEAD_DIM + (first + g) * HEAD_DIM, HEAD_DIM)
            for g in range(HEADS_DOT)
        ]
        queries = jnp.concatenate(
            [jnp.concatenate([q_ref[:, pl.ds(c, HEAD_DIM)], eye], 1) for c in cols], 0
        )
        scores = lax.dot_general(
            queries, keys, (((1,), (1,)), ((), ())), preferred_element_type=jnp.float32
        )
        peak = jnp.max(scores, axis=1, keepdims=True)
        weights = jnp.exp2((scores - peak) * factor).astype(jnp.bfloat16)
        summed = jnp.dot(weights, values, preferred_element_type=jnp.float32)
        mixed = (summed[:, :HEAD_DIM] / summed[:, HEAD_DIM:]).astype(jnp.bfloat16)
        for g, c in enumerate(cols):
            out_ref[:, pl.ds(c, HEAD_DIM)] = mixed[g * rows : (g + 1) * rows]


def kernel(
    q_now, stash_now, pos_now, q_old, pos_old, kept, held,
    mixed_now, mixed_old, stored,
    qn, qo, kv_now, kv_old, mask_now, mask_old, eye,
    load_sem, send_sem, recv_sem, go_sem,
):
    rows = stash_now.shape[0]
    half = kept.shape[0]
    part = half // CHUNKS
    sections = lax.axis_size("section")
    count = lax.axis_size("tp")
    s = lax.axis_index("section")
    t = lax.axis_index("tp")
    mirror = {"section": sections - 1 - s}
    right = {"tp": t + 1}
    has_right = t < count - 1
    has_left = t > 0
    seam = count // 2
    gives_direct = t == seam - 1
    takes_direct = t == seam
    tells = t == seam - 2
    forwards_first = (t == 0) | (t == seam)
    passes_on = has_right & jnp.logical_not(gives_direct)
    takes_passed = has_left & jnp.logical_not(takes_direct)

    loads = [
        pltpu.make_async_copy(stash_now, kv_now.at[pl.ds(rows, rows)], load_sem.at[0]),
        pltpu.make_async_copy(q_now, qn, load_sem.at[1]),
        pltpu.make_async_copy(kept, kv_old.at[pl.ds(rows, half)], load_sem.at[2]),
        pltpu.make_async_copy(q_old, qo, load_sem.at[3]),
    ]
    for load in loads:
        load.start()

    barrier = pltpu.get_barrier_semaphore()
    pl.semaphore_signal(
        barrier, inc=1,
        device_id={"section": sections - 1 - s, "tp": t - gives_direct.astype(jnp.int32)},
        device_id_type=MESH,
    )

    @pl.when(has_left)
    def _():
        pl.semaphore_signal(barrier, inc=1, device_id={"tp": t - 1}, device_id_type=MESH)

    @pl.when(takes_direct)
    def _():
        pl.semaphore_signal(
            barrier, inc=1, device_id={"section": sections - 1 - s, "tp": t - 1}, device_id_type=MESH
        )

    pl.semaphore_wait(
        barrier, 1 + has_right.astype(jnp.int32) + tells.astype(jnp.int32)
    )

    @pl.when(tells)
    def _():
        pl.semaphore_signal(go_sem, inc=1, device_id=right, device_id_type=MESH)

    def remote(index, src, dst, device):
        return pltpu.make_async_remote_copy(
            src_ref=src, dst_ref=dst, send_sem=send_sem.at[index], recv_sem=recv_sem.at[index],
            device_id=device, device_id_type=MESH,
        )

    swap = [
        remote(
            c, held.at[pl.ds(c * part, part)],
            kv_old.at[pl.ds(rows + half + c * part, part)], mirror,
        )
        for c in range(CHUNKS)
    ]
    pass_on = [
        remote(
            CHUNKS + c, kv_old.at[pl.ds(rows + half + c * part, part)],
            kv_old.at[pl.ds(half + c * part, part)], right,
        )
        for c in range(CHUNKS)
    ]
    shift_now = remote(2 * CHUNKS, stash_now, kv_now.at[pl.ds(0, rows)], right)
    shift_kept = remote(2 * CHUNKS + 1, kept, kv_old.at[pl.ds(0, half)], right)
    direct = remote(
        2 * CHUNKS + 3, held, kv_old.at[pl.ds(half, half)],
        {"section": sections - 1 - s, "tp": t + 1},
    )
    evict = remote(2 * CHUNKS + 2, stash_now.at[pl.ds(rows - half, half)], stored, mirror)

    @pl.when(jnp.logical_not(gives_direct))
    def _():
        for copy in swap:
            copy.start()

    @pl.when(gives_direct)
    def _():
        direct.start()

    @pl.when(has_right)
    def _():
        shift_now.start()
        shift_kept.start()

    @pl.when(gives_direct)
    def _():
        pl.semaphore_wait(go_sem, 1)
        for copy in swap:
            copy.start()

    evict.start()

    @pl.when(jnp.logical_not(has_left))
    def _():
        kv_now[pl.ds(0, rows), :] = jnp.zeros((rows, 2 * KV_WIDTH), jnp.bfloat16)
        kv_old[pl.ds(0, rows), :] = jnp.zeros((rows, 2 * KV_WIDTH), jnp.bfloat16)

    eye[...] = jnp.where(
        lax.broadcasted_iota(jnp.int32, (rows, rows), 0)
        == lax.broadcasted_iota(jnp.int32, (rows, rows), 1),
        1.0, 0.0,
    ).astype(jnp.bfloat16)
    mask_now[...] = mask_rows(pos_now[...], rows)
    mask_old[...] = mask_rows(pos_old[...], rows)

    @pl.when(forwards_first)
    def _():
        for c in range(CHUNKS):
            swap[c].wait_recv()
            pass_on[c].start()

    loads[0].wait()
    loads[1].wait()

    @pl.when(has_left)
    def _():
        shift_now.wait_recv()

    for head in range(KV_HEADS):
        attend_head(head, qn, kv_now, mask_now, eye, mixed_now)
        for c in range(head * CHUNKS // KV_HEADS, (head + 1) * CHUNKS // KV_HEADS):

            @pl.when(jnp.logical_not(forwards_first))
            def _(c=c):
                swap[c].wait_recv()

            @pl.when(passes_on & jnp.logical_not(forwards_first))
            def _(c=c):
                pass_on[c].start()

    loads[2].wait()
    loads[3].wait()

    @pl.when(has_left)
    def _():
        shift_kept.wait_recv()

    @pl.when(takes_passed)
    def _():
        for copy in pass_on:
            copy.wait_recv()

    @pl.when(takes_direct)
    def _():
        direct.wait_recv()

    for head in range(KV_HEADS):
        attend_head(head, qo, kv_old, mask_old, eye, mixed_old)

    for copy in swap:
        copy.wait_send()

    @pl.when(has_right)
    def _():
        shift_now.wait_send()
        shift_kept.wait_send()

    @pl.when(passes_on)
    def _():
        for copy in pass_on:
            copy.wait_send()

    @pl.when(gives_direct)
    def _():
        direct.wait_send()

    evict.wait()


def write_out(now_in, old_in, stored_in, now_out, old_out, stored_out, sem):
    copies = [
        pltpu.make_async_copy(now_in, now_out, sem.at[0]),
        pltpu.make_async_copy(old_in, old_out, sem.at[1]),
        pltpu.make_async_copy(stored_in, stored_out, sem.at[2]),
    ]
    for copy in copies:
        copy.start()
    for copy in copies:
        copy.wait()


def body(queries_now, stash_now, positions_now, queries_old, positions_old, stash_kept, stash_held):
    rows, width = queries_now.shape[1:]
    half, kv_width = stash_kept.shape[1:]
    bf16 = jnp.bfloat16
    hbm = pl.BlockSpec(memory_space=pl.ANY)
    vmem = pl.BlockSpec(memory_space=pltpu.VMEM)
    remote_count = 2 * CHUNKS + 4
    mixed_now, mixed_old, stored = pl.pallas_call(
        kernel,
        out_shape=(
            pltpu.VMEM((rows, width), bf16),
            pltpu.VMEM((rows, width), bf16),
            pltpu.VMEM((half, kv_width), bf16),
        ),
        in_specs=[hbm, hbm, vmem, hbm, vmem, hbm, hbm],
        out_specs=(vmem, vmem, vmem),
        scratch_shapes=[
            pltpu.VMEM((rows, width), bf16),
            pltpu.VMEM((rows, width), bf16),
            pltpu.VMEM((2 * rows, kv_width), bf16),
            pltpu.VMEM((2 * rows, kv_width), bf16),
            pltpu.VMEM((2 * rows, rows), bf16),
            pltpu.VMEM((2 * rows, rows), bf16),
            pltpu.VMEM((rows, rows), bf16),
            pltpu.SemaphoreType.DMA((4,)),
            pltpu.SemaphoreType.DMA((remote_count,)),
            pltpu.SemaphoreType.DMA((remote_count,)),
            pltpu.SemaphoreType.REGULAR,
        ],
        compiler_params=pltpu.CompilerParams(collective_id=0, has_side_effects=True),
        name="relay_attention",
    )(
        queries_now[0], stash_now[0], positions_now, queries_old[0], positions_old,
        stash_kept[0], stash_held[0],
    )
    shapes = tuple(jax.ShapeDtypeStruct(a.shape, a.dtype) for a in (mixed_now, mixed_old, stored))
    mixed_now, mixed_old, stored = pl.pallas_call(
        write_out,
        out_shape=shapes,
        in_specs=[pl.BlockSpec(memory_space=pl.ANY)] * 3,
        out_specs=(hbm, hbm, hbm),
        scratch_shapes=[pltpu.SemaphoreType.DMA((3,))],
        compiler_params=pltpu.CompilerParams(vmem_limit_bytes=2**20),
        name="write_out",
    )(mixed_now, mixed_old, stored)
    return (mixed_now[None], mixed_old[None], stored[None])


def solution(mesh):
    return jax.shard_map(
        body,
        mesh=mesh,
        in_specs=(
            P("section", "tp", None),
            P("section", "tp", None),
            P("section", "tp"),
            P("section", "tp", None),
            P("section", "tp"),
            P("section", "tp", None),
            P("section", "tp", None),
        ),
        out_specs=(P("section", "tp", None), P("section", "tp", None), P("section", "tp", None)),
        check_vma=False,
    )
```
